32 devices in a mesh: dp: 4 (over y, core), expert: 8 (over z, x).
Axes of the slice: x: 2, y: 2, z: 4, core: 2. Of those that a mesh axis runs over, the one named last changes fastest.
Arguments:
- tokens: bfloat16 [4096, 2048], P(('dp', 'expert')), may hold values from -6 to 6
- expert_ids: int32 [4096, 4], P(('dp', 'expert')), may hold values from 0 to 31, as said below
- gate_weights: float32 [4096, 4], P(('dp', 'expert')), may hold values from 0.02 to 0.5
- w_gate: bfloat16 [32, 2048, 768], P('expert', 'dp'), may hold values from -0.125 to 0.125
- w_up: bfloat16 [32, 2048, 768], P('expert', 'dp'), may hold values from -0.125 to 0.125
- w_down: bfloat16 [32, 768, 2048], P('expert', None, 'dp'), may hold values from -0.21875 to 0.21875
Outputs:
- combined: bfloat16 [4096, 2048], P(('dp', 'expert'))
The draws below stay inside these ranges and needn't reach their ends.
Inputs may be any that keep to these rules, and one draw needn't show every extreme that they name: `expert_ids`: each row names 4 different experts. The rows of one device name no expert more than 24 times; in every dp group two experts are named exactly 24 times by the rows of each of its devices.
All inputs are finite; a program needn't handle non-finite values.
Results may differ from the reference program's by a relative error of at most 0.0057.
Values may be sent and summed in bfloat16 or wider, within the bound.
No kernel may reach another device: no remote copies, remote signals or barrier semaphores. Data moves between devices by JAX's collectives and lax.ppermute only.
A program may use at most 128 MiB of HBM per device.

```python
import math
import jax
import jax.numpy as jnp
from jax import lax

D = 2048
FF = 768
TOP = 4
EXPERTS = 32
TOK_DEV = 128
CAPACITY = 24
GROUP_TOK = 1024
TOKENS = 4096
N_DP = 4


def draw_expert_ids(key, part):
    devices = TOKENS // TOK_DEV
    per_group = GROUP_TOK // TOK_DEV
    groups = TOKENS // GROUP_TOK
    cold_count = EXPERTS - 2
    base_key = jax.random.fold_in(key, 17)
    hot_key, device_key = jax.random.split(base_key)

    def group_order(group_key):
        return jax.random.permutation(group_key, EXPERTS).astype(jnp.int32)
    group_perms = jax.vmap(group_order)(jax.random.split(hot_key, groups))

    def device_rows(dev_key, device):
        order = lax.dynamic_index_in_dim(group_perms, device // per_group, 0, keepdims=False)
        cold_key, token_key, column_key = jax.random.split(dev_key, 3)
        cold_perm = jax.random.permutation(cold_key, cold_count).astype(jnp.int32)
        cold_list = order[2:][cold_perm]
        token_rank = jax.random.permutation(token_key, TOK_DEV).astype(jnp.int32)
        is_hot = token_rank < 2 * CAPACITY
        hot_pick = jnp.where(token_rank < CAPACITY, order[0], order[1])
        start = token_rank * (TOP - 1) + jnp.maximum(token_rank - 2 * CAPACITY, 0)
        offsets = jnp.arange(TOP, dtype=jnp.int32)
        positions = (start[:, None] + offsets[None, :]) % cold_count
        cold_pick = cold_list[positions]
        hot_row = jnp.concatenate([hot_pick[:, None], cold_pick[:, :TOP - 1]], axis=1)
        chosen = jnp.where(is_hot[:, None], hot_row, cold_pick)
        scores = jax.random.randint(column_key, (TOK_DEV, TOP), 0, 1 << 20, dtype=jnp.int32) * TOP
        scores = scores + jnp.arange(TOP, dtype=jnp.int32)[None, :]
        column_order = jnp.argsort(scores, axis=1)
        return jnp.take_along_axis(chosen, column_order, axis=1)
    all_rows = jax.vmap(device_rows)(jax.random.split(device_key, devices), jnp.arange(devices, dtype=jnp.int32))
    return all_rows.reshape(TOKENS, TOP).astype(jnp.int32)


def steps_of(own_key, extent, pieces, smallest, high):
    def one(dim, blocks):
        heights = jax.random.uniform(jax.random.fold_in(jax.random.fold_in(own_key, 6), dim), (blocks,), jnp.float32, smallest / len(pieces), high / len(pieces))
        return jnp.repeat(jnp.exp(heights), extent[dim] // blocks).reshape((-1,) + (1,) * (len(extent) - dim - 1))

    factor_of = one(*pieces[0])
    for cut in pieces[1:]:
        factor_of = factor_of * one(*cut)
    return factor_of


def bell_draw(key, dims, spread, bound, cuts=(), held_as=jnp.bfloat16):
    drawn = jax.random.normal(key, dims, jnp.float32) * spread
    if len(cuts) > 0:
        drawn = steps_of(key, dims, cuts, -0.22, 0.18) * drawn
    return jnp.clip(drawn, min=-bound, max=bound).astype(held_as)


def setup_inputs(seed: int = 0) -> dict:
    seeds = jax.random.split(jax.random.key(seed), 7)
    return {
        "tokens": bell_draw(seeds[0], (TOKENS, D), 1.0, 6.0, ((0, 32),)),
        "expert_ids": draw_expert_ids(jax.random.fold_in(seeds[6], 71), 0),
        "gate_weights": jnp.clip(jnp.exp(math.log(0.5) - 3.218876 * jax.random.uniform(seeds[2], (TOKENS, TOP), jnp.float32) ** steps_of(seeds[2], (TOKENS, TOP), ((0, 32),), -0.2, 0.2)), 0.02, 0.5),
        "w_gate": bell_draw(seeds[3], (EXPERTS, D, FF), D ** -0.5, 0.125, ((0, 8), (1, 4))),
        "w_up": bell_draw(seeds[4], (EXPERTS, D, FF), D ** -0.5, 0.125, ((0, 8), (1, 4))),
        "w_down": bell_draw(seeds[5], (EXPERTS, FF, D), FF ** -0.5, 0.21875, ((0, 8), (2, 4))),
    }


def expert_layer(token_rows, gate_matrix, up_matrix, down_matrix):
    gate_sum = jnp.dot(token_rows, gate_matrix, preferred_element_type=jnp.float32)
    up_sum = jnp.dot(token_rows, up_matrix, preferred_element_type=jnp.float32)
    hidden = (jax.nn.silu(gate_sum) * up_sum).astype(jnp.bfloat16)
    return jnp.dot(hidden, down_matrix, preferred_element_type=jnp.float32).astype(jnp.bfloat16)


def reference(tokens, expert_ids, gate_weights, w_gate, w_up, w_down):
    group_tokens = tokens.reshape(N_DP, GROUP_TOK, D)
    group_ids = expert_ids.reshape(N_DP, GROUP_TOK, TOP)
    group_gates = gate_weights.reshape(N_DP, GROUP_TOK, TOP)
    row_limit = CAPACITY * (GROUP_TOK // TOK_DEV)

    def one_group(packed):
        token_block, id_block, gate_block = packed

        def one_expert(running, expert_id):
            hit_mask = id_block == expert_id
            named_rows = jnp.any(hit_mask, axis=1)
            row_weight = jnp.sum(jnp.where(hit_mask, gate_block, jnp.zeros_like(gate_block)), axis=1)
            row_index = jnp.nonzero(named_rows, size=row_limit, fill_value=0)[0].astype(jnp.int32)
            live_rows = jnp.arange(row_limit, dtype=jnp.int32) < jnp.sum(named_rows.astype(jnp.int32))
            selected = token_block[row_index]
            result = expert_layer(selected, w_gate[expert_id], w_up[expert_id], w_down[expert_id])
            weighted = row_weight[row_index][:, None] * result.astype(jnp.float32)
            weighted = jnp.where(live_rows[:, None], weighted, jnp.zeros_like(weighted))
            return running.at[row_index].add(weighted), None

        start_sum = jnp.zeros((GROUP_TOK, D), jnp.float32)
        totals, _ = lax.scan(one_expert, start_sum, jnp.arange(EXPERTS, dtype=jnp.int32))
        return totals.astype(jnp.bfloat16)

    combined = lax.map(one_group, (group_tokens, group_ids, group_gates))
    return combined.reshape(TOKENS, D)
```

```python
import functools

import jax
import jax.numpy as jnp
from jax import lax
from jax.experimental import pallas as pl
from jax.experimental.pallas import tpu as pltpu
from jax.sharding import PartitionSpec as P

BF16 = jnp.bfloat16
F32 = jnp.float32


def expert_layer(expert_rows, gate_full, up_full, down_full):
    gate_sum = jnp.einsum(
        "erd,edf->erf", expert_rows, gate_full, preferred_element_type=jnp.float32
    )
    up_sum = jnp.einsum("erd,edf->erf", expert_rows, up_full, preferred_element_type=jnp.float32)
    hidden = (jax.nn.silu(gate_sum) * up_sum).astype(jnp.bfloat16)
    return jnp.einsum("erf,efd->erd", hidden, down_full, preferred_element_type=jnp.float32).astype(
        jnp.bfloat16
    )


def gathered_weights(tokens, expert_ids, gate_weights, w_gate, w_up, w_down):
    members = lax.axis_size("expert")
    tok_count = tokens.shape[0]
    model_width = tokens.shape[1]
    top_count = expert_ids.shape[1]
    local_experts = w_gate.shape[0]
    capacity = tok_count * 3 // 16
    total_experts = members * local_experts
    buffer_rows = total_experts * capacity
    flat_ids = expert_ids.reshape(-1)
    one_hot = (flat_ids[:, None] == jnp.arange(total_experts, dtype=jnp.int32)[None, :]).astype(
        jnp.int32
    )
    earlier = jnp.cumsum(one_hot, axis=0) - one_hot
    slot_index = jnp.sum(earlier * one_hot, axis=1)
    owner_dev = flat_ids // local_experts
    local_index = flat_ids % local_experts
    target = (local_index * members + owner_dev) * capacity + slot_index
    token_of = jnp.arange(flat_ids.shape[0], dtype=jnp.int32) // top_count
    source_row = jnp.zeros((buffer_rows,), jnp.int32).at[target].set(token_of)
    filled = jnp.zeros((buffer_rows,), jnp.bool_).at[target].set(True)
    outgoing = jnp.where(filled[:, None], tokens[source_row], jnp.zeros((), tokens.dtype))
    outgoing = outgoing.reshape(local_experts, members, capacity, model_width)
    incoming = lax.all_to_all(outgoing, "expert", split_axis=1, concat_axis=1, tiled=True)
    expert_rows = incoming.reshape(local_experts, members * capacity, model_width)
    gate_full, up_full = (
        lax.all_gather(w_gate, "dp", axis=1, tiled=True),
        lax.all_gather(w_up, "dp", axis=1, tiled=True),
    )
    down_full = lax.all_gather(w_down, "dp", axis=2, tiled=True)
    results = expert_layer(expert_rows, gate_full, up_full, down_full)
    returned = lax.all_to_all(
        results.reshape(local_experts, members, capacity, model_width),
        "expert",
        split_axis=1,
        concat_axis=1,
        tiled=True,
    )
    flat_back = returned.reshape(buffer_rows, model_width)
    picked = flat_back[target].reshape(tok_count, top_count, model_width).astype(jnp.float32)
    combined = jnp.sum(gate_weights[:, :, None] * picked, axis=1)
    return combined.astype(jnp.bfloat16)


def slots_of(info_refs, base, top, experts, cap):
    hits = []
    for g in range(2):
        for ref in info_refs:
            ids = ref[g, :top, :]
            for e in range(experts):
                want = (base + e).astype(F32)
                hits.append(jnp.max(jnp.where(ids == want, 1.0, 0.0), axis=0, keepdims=True))
    hit = jnp.concatenate(hits, axis=0)
    tok = hit.shape[1]
    before = lax.broadcasted_iota(jnp.int32, (tok, tok), 0) < lax.broadcasted_iota(
        jnp.int32, (tok, tok), 1
    )
    order = jnp.dot(
        hit.astype(BF16), jnp.where(before, 1.0, 0.0).astype(BF16), preferred_element_type=F32
    )
    slots = {}
    at = 0
    for g in range(2):
        for s in range(len(info_refs)):
            for e in range(experts):
                row = jnp.where(hit[at : at + 1] > 0.5, order[at : at + 1] + float(s * cap), -1.0)
                slots[g, s, e] = row.astype(jnp.int32)
                at += 1
    return slots


def rows_kernel(
    cap, top, place, info_a, info_b, tok_a, tok_b, wg_own, wg_oth, wu_own, wu_oth,
    send, keep, rows,
):
    core, base = place[0], place[1]
    e = pl.program_id(0)
    experts = rows.shape[0]
    both = 2 * cap
    quarter = wg_own.shape[1]
    width = wg_own.shape[2]

    @pl.when(e == 0)
    def _():
        slots = slots_of((info_a, info_b), base, top, experts, cap)
        tok = tok_a.shape[1]
        row_id = lax.broadcasted_iota(jnp.int32, (both, tok), 0)
        for g in range(2):
            total = None
            for s, tref in enumerate((tok_a, tok_b)):
                pick = jnp.concatenate(
                    [jnp.where(row_id == slots[g, s, q], 1.0, 0.0) for q in range(experts)], axis=0
                ).astype(BF16)
                part = jnp.dot(pick, tref[g], preferred_element_type=F32)
                total = part if total is None else total + part
            total = total.astype(BF16)
            for q in range(experts):
                rows[q, g * both : (g + 1) * both, :] = total[q * both : (q + 1) * both]

    own = rows[e, :, pl.ds(pl.multiple_of(core * quarter, quarter), quarter)]
    oth = rows[e, :, pl.ds(pl.multiple_of((1 - core) * quarter, quarter), quarter)]
    for at, (wo, wt) in enumerate(((wg_own, wg_oth), (wu_own, wu_oth))):
        total = jnp.dot(own, wo[0], preferred_element_type=F32) + jnp.dot(
            oth, wt[0], preferred_element_type=F32
        )
        keep[0, :, at * width : (at + 1) * width] = total[:both]
        send[0, :, at * width : (at + 1) * width] = total[both:].astype(BF16)


def down_kernel(
    cap, top, place, info_a, info_b, hid_own, hid_par, wd_own, wd_oth, send, keep, outs
):
    core, base = place[0], place[1]
    e = pl.program_id(0)
    experts = pl.num_programs(0)
    both = 2 * cap
    quarter = wd_own.shape[2]
    hid = jnp.concatenate([hid_own[0], hid_par[0]], axis=0)
    for col, w in ((core, wd_own), (1 - core, wd_oth)):
        out = jnp.dot(hid, w[0], preferred_element_type=F32).astype(BF16)
        cols = pl.ds(pl.multiple_of(col * quarter, quarter), quarter)
        at = pl.ds(pl.multiple_of(e * both, both), both)
        outs[0, at, cols] = out[:both]
        outs[1, at, cols] = out[both:]

    @pl.when(e == experts - 1)
    def _():
        count = outs.shape[1] // both
        slots = slots_of((info_a, info_b), base, top, count, cap)
        tok = info_a.shape[2]
        row_id = lax.broadcasted_iota(jnp.int32, (both, tok), 0)
        for g in range(2):
            for s, (ref, dest) in enumerate(((info_a, keep), (info_b, send))):
                ids = ref[g, :top, :]
                scale = ref[g, top : 2 * top, :]
                parts = []
                for q in range(count):
                    want = (base + q).astype(F32)
                    weight = jnp.sum(jnp.where(ids == want, scale, 0.0), axis=0, keepdims=True)
                    parts.append(jnp.where(row_id == slots[g, s, q], weight, 0.0))
                spread = jnp.concatenate(parts, axis=0)
                high = spread.astype(BF16)
                low = (spread - high.astype(F32)).astype(BF16)
                dims = (((0,), (0,)), ((), ()))
                total = lax.dot_general(high, outs[g], dims, preferred_element_type=F32)
                total = total + lax.dot_general(low, outs[g], dims, preferred_element_type=F32)
                dest[g] = total.astype(dest.dtype)


def whole(shape):
    return pl.BlockSpec(shape, lambda e, place: (0,) * len(shape))


def slab(shape):
    return pl.BlockSpec((1,) + tuple(shape[1:]), lambda e, place: (e,) + (0,) * (len(shape) - 1))


def call(kernel, name, grid, place, fulls, slabs, outs_full, outs_slab, scratch, flops):
    operands = fulls + slabs
    out_shape = outs_full + outs_slab
    moved = sum(a.size * a.dtype.itemsize for a in operands) + sum(
        a.size * jnp.dtype(a.dtype).itemsize for a in out_shape
    )
    return pl.pallas_call(
        kernel,
        name=name,
        out_shape=out_shape,
        grid_spec=pltpu.PrefetchScalarGridSpec(
            num_scalar_prefetch=1,
            grid=(grid,),
            in_specs=[whole(a.shape) for a in fulls] + [slab(a.shape) for a in slabs],
            out_specs=[whole(a.shape) for a in outs_full] + [slab(a.shape) for a in outs_slab],
            scratch_shapes=scratch,
        ),
        compiler_params=pltpu.CompilerParams(dimension_semantics=("arbitrary",)),
        cost_estimate=pl.CostEstimate(flops=flops, bytes_accessed=moved, transcendentals=0),
    )(place, *operands)


def local_weights(tokens, expert_ids, gate_weights, w_gate, w_up, w_down):
    members = lax.axis_size("expert")
    planes = members // 2
    tok, width = tokens.shape
    top = expert_ids.shape[1]
    experts, quarter, hidden_width = w_gate.shape
    half = 2 * quarter
    cap = tok * 3 // 16
    both = 2 * cap
    i = lax.axis_index("dp")
    j = lax.axis_index("expert")
    side, core = i // 2, i % 2
    place = jnp.stack([core, j * experts]).astype(jnp.int32)

    def across(x):
        return lax.ppermute(x, "dp", [(d, d ^ 2) for d in range(4)])

    def cores(x):
        return lax.ppermute(x, "dp", [(d, d ^ 1) for d in range(4)])

    def flip(x):
        return lax.ppermute(x, "expert", [(m, m ^ 1) for m in range(members)])

    def plane(x, k):
        return lax.ppermute(x, "expert", [(m, m ^ (2 * k)) for m in range(members)])

    info = jnp.concatenate([expert_ids.astype(F32).T, gate_weights.T], axis=0)
    away = across(lax.dynamic_slice(tokens, (0, (1 - side) * half), (tok, half)))
    info_y = across(info)
    mine = lax.dynamic_slice(tokens, (0, side * half), (tok, half))
    block0 = jnp.stack([mine, away])
    info0 = jnp.stack([info, info_y])
    wg_oth, wu_oth, wd_oth = cores(w_gate), cores(w_up), cores(w_down)
    info_a = [info0] + [plane(info0, k) for k in range(1, planes)]
    tok_a = [block0] + [plane(block0, k) for k in range(1, planes)]
    info_flip = flip(jnp.stack(info_a))

    kept = None
    returned = []
    for k in range(planes):
        tok_b = flip(tok_a[k])
        info_b = info_flip[k]
        send, keep = call(
            functools.partial(rows_kernel, cap, top),
            "gate_up",
            experts,
            place,
            [info_a[k], info_b, tok_a[k], tok_b],
            [w_gate, wg_oth, w_up, wu_oth],
            [],
            [
                jax.ShapeDtypeStruct((experts, both, 2 * hidden_width), BF16),
                jax.ShapeDtypeStruct((experts, both, 2 * hidden_width), F32),
            ],
            [pltpu.VMEM((experts, 2 * both, half), BF16)],
            4 * experts * 2 * both * half * hidden_width,
        )
        sums = keep + across(send).astype(F32)
        gate_sum, up_sum = sums[..., :hidden_width], sums[..., hidden_width:]
        hidden = (jax.nn.silu(gate_sum) * up_sum).astype(BF16)
        hidden_par = across(hidden)
        back, stay = call(
            functools.partial(down_kernel, cap, top),
            "down",
            experts,
            place,
            [info_a[k], info_b],
            [hidden, hidden_par, w_down, wd_oth],
            [
                jax.ShapeDtypeStruct((2, tok, half), BF16),
                jax.ShapeDtypeStruct((2, tok, half), F32),
            ],
            [],
            [pltpu.VMEM((2, experts * both, half), BF16)],
            2 * experts * 2 * both * half * hidden_width,
        )
        part = stay + flip(back).astype(F32)
        if k == 0:
            kept = part
        else:
            returned.append(plane(part.astype(BF16), k))
    total = kept
    for r in returned:
        total = total + r.astype(F32)
    total = total.astype(BF16)
    far = across(total[1])
    near = total[0]
    first = jnp.where(side == 0, near, far)
    second = jnp.where(side == 0, far, near)
    return jnp.concatenate([first, second], axis=1)


def solution(mesh):
    in_specs = (
        P(("dp", "expert"), None),
        P(("dp", "expert"), None),
        P(("dp", "expert"), None),
        P("expert", "dp", None),
        P("expert", "dp", None),
        P("expert", None, "dp"),
    )
    out_specs = P(("dp", "expert"), None)
    planes = mesh.shape["expert"] // 2
    paired = mesh.shape["dp"] == 4 and planes >= 1 and planes & (planes - 1) == 0
    return jax.shard_map(
        local_weights if paired else gathered_weights,
        mesh=mesh,
        in_specs=in_specs,
        out_specs=out_specs,
        check_vma=False,
    )
```
